32 devices in a mesh: rep: 2 (over y), ep: 8 (over z, core), tp: 2 (over x).
Axes of the slice: x: 2, y: 2, z: 4, core: 2. Of those that a mesh axis runs over, the one named last changes fastest.
Arguments:
- hidden_states: bfloat16 [2, 1024, 2048], P(None, ('rep', 'ep'), 'tp'), parts along dimension 1, may hold values from -8 to 8
- queries: bfloat16 [2, 1024, 4096], P(None, ('rep', 'ep'), 'tp'), parts along dimension 1, may hold values from -8 to 8
- fresh_key_value: bfloat16 [2, 1024, 2, 512], P(None, ('rep', 'ep'), None, 'tp'), parts along dimension 1, may hold values from -8 to 8
- cache: bfloat16 [16, 2, 1024, 512], P(('rep', 'ep'), None, None, 'tp'), parts along dimension 0, may hold values from -8 to 8
- cache_lengths: int32 [16], P(('rep', 'ep')), parts along dimension 0, may hold values from 1 to 1024, 4096 in all
- out_weight: bfloat16 [4096, 2048], P('tp', 'ep'), may hold values from -1 to 1
- router_weight: bfloat16 [2048, 16], P('tp'), may hold values from -0.125 to 0.125
- expert_weights: bfloat16 [16, 3, 2048, 384], P('ep', None, 'tp'), may hold values from -0.21875 to 0.21875
- expert_ids: int32 [2, 1024, 8], P(None, ('rep', 'ep')), parts along dimension 1, may hold values from 0 to 15, all different within a row; in each aligned block of 64 rows (0 to 63, 64 to 127, ..., all dimensions but the last counted through in order) at most 48 rows name the same one
- old_slots: int32 [16], replicated, may hold values from 0 to 15, as said below
- new_slots: int32 [16], replicated, may hold values from 0 to 15, as said below
- moved_experts: int32 [4], replicated, may hold values from 0 to 15, as said below
Outputs:
- mixed: bfloat16 [2, 1024, 2048], P(None, ('rep', 'ep'), 'tp'), parts along dimension 1
The draws below stay inside these ranges and needn't reach their ends.
There are 2 independent parts, one for each index of `rep`. The reference program is written for one: setup_inputs(seed, part) draws one part's arguments, and reference() takes and returns one part's arrays. A program takes and returns all parts, laid end to end along the dimension named above; an argument that names none is the same for every part. Nothing has to cross between parts.
Inputs may be any that keep to these rules, and one draw needn't show every extreme that they name: `expert_ids`: each row names 8 different experts. Within the 64 rows of one request in one token block, no expert is named by more than 48 rows, a bound that some block reaches. `old_slots`: A permutation: each slot holds one expert. `new_slots`: equal to old_slots except at the moved experts, which take one another's old slots, none keeping its own. `moved_experts`: 4 different experts; no two of their old slots s share the same s // 2.
All inputs are finite; a program needn't handle non-finite values. No bound on the sum of `cache_lengths` on one device may be relied on, other than what follows from the above.
Results may differ from the reference program's by a relative error of at most 0.017.
Values may be sent and summed in bfloat16 or wider, within the bound.
A program may use at most 64 MiB of HBM per device.

```python
import math
import jax
import jax.numpy as jnp
import numpy as np
from jax import lax

D = 2048
QUERY_HEADS = 32
KEY_VALUE_HEADS = 4
HEAD_SIZE = 128
FFW = 384
TOP = 8
EXP_DEV = 2
REQUEST_TOKENS = 64
CACHED_POSITIONS = 1024
EXPERTS = 16
REQUEST_COUNT = 8
BLOCK_TOKENS = 512
CAP = 48
MOVED = 4
QUARTER = 1024
N_TP = 2


def slot_plan(key):
    base_key = jax.random.fold_in(key, 5)
    perm_key, device_key, local_key = jax.random.split(base_key, 3)
    old_table = jax.random.permutation(perm_key, EXPERTS).astype(jnp.int32)
    devices = jax.random.permutation(device_key, REQUEST_COUNT)[:MOVED].astype(jnp.int32)
    local_pick = jax.random.randint(local_key, (MOVED,), 0, EXP_DEV).astype(jnp.int32)
    chosen = (devices * EXP_DEV + local_pick).astype(jnp.int32)
    owners = jnp.argsort(old_table).astype(jnp.int32)
    moved_list = owners[chosen].astype(jnp.int32)
    new_table = old_table.at[moved_list].set(jnp.roll(chosen, -1))
    return (old_table, new_table, moved_list)


def draw_old_slots(key, part):
    return slot_plan(key)[0]


def draw_new_slots(key, part):
    return slot_plan(key)[1]


def draw_moved_experts(key, part):
    return slot_plan(key)[2]


def draw_queries(key, part):
    array_extent = (2, BLOCK_TOKENS, QUERY_HEADS * HEAD_SIZE)
    return jnp.clip(jax.random.normal(jax.random.fold_in(key, 1), array_extent), -8.0, 8.0).astype(jnp.bfloat16)


def draw_fresh_key_value(key, part):
    array_extent = (2, BLOCK_TOKENS, 2, KEY_VALUE_HEADS * HEAD_SIZE)
    return jnp.clip(jax.random.normal(jax.random.fold_in(key, 2), array_extent), -8.0, 8.0).astype(jnp.bfloat16)


def draw_hidden_states(key, part):
    array_extent = (2, BLOCK_TOKENS, D)
    along = jnp.arange(D, dtype=jnp.float32) / (D - 1)
    rough = jnp.exp(jax.random.uniform(jax.random.fold_in(key, 8), (D,), minval=jnp.log(0.7), maxval=jnp.log(1.4)))
    base_values = jax.random.normal(jax.random.fold_in(key, 4), array_extent)
    row_scale = jnp.exp(jax.random.uniform(jax.random.fold_in(key, 7), (2, BLOCK_TOKENS, 1), minval=jnp.log(0.2), maxval=jnp.log(2.0)))
    column_scale = jnp.exp(jnp.log(0.4) + (jnp.log(4.0) - jnp.log(0.4)) * along) * rough
    return jnp.clip(0.5 * base_values * row_scale * column_scale, -8.0, 8.0).astype(jnp.bfloat16)


def level_of(key, dims, cuts, least, high):
    def one(dim, blocks):
        draws = jax.random.uniform(jax.random.fold_in(jax.random.fold_in(key, 6), dim), (blocks,), jnp.float32, least / len(cuts), high / len(cuts))
        return jnp.repeat(jnp.exp(draws), dims[dim] // blocks).reshape((-1,) + (1,) * (len(dims) - dim - 1))

    gain = one(*cuts[0])
    for cut in cuts[1:]:
        gain = gain * one(*cut)
    return gain


def profile(number_of, total, bound, skew):
    portions = [(1 << 20) // math.isqrt(grade ** skew) + 1 for grade in range(2, number_of + 1)]
    spare, counts = total - bound - (number_of - 1), [1] * (number_of - 1)
    while spare > 0:
        candidates = [i for i in range(number_of - 1) if counts[i] < bound]
        mass, remaining = sum([portions[i] for i in candidates]), spare
        for i in candidates:
            more = min(bound - counts[i], max(1, remaining * portions[i] // mass), spare)
            counts[i] = counts[i] + more
            spare = spare - more
    return np.array([bound] + counts)


def ragged_sizes(rng, count, total, bound, lean):
    if count == 2:
        one = jax.random.randint(rng, (), max(1, total - bound), min(bound, total - 1) + 1)
        return jnp.stack([one, total - one])
    sizes = jnp.asarray(profile(count, total, bound, lean), jnp.int32)
    twos = (count - 1) // 2
    giver, receiver = sizes[1:1 + 2 * twos:2], sizes[2:2 + 2 * twos:2]
    margin = jnp.minimum(giver - 1, bound - receiver)
    shifted = jax.random.randint(jax.random.fold_in(rng, 1), (twos,), 0, 1 << 20) % (margin + 1)
    sizes = sizes.at[1:1 + 2 * twos:2].set(giver - shifted).at[2:2 + 2 * twos:2].set(receiver + shifted)
    return sizes[jax.random.permutation(jax.random.fold_in(rng, 2), count)]


def deal_out(rng, own, number, rows, amount, top, most, lean):
    sequence = jax.random.permutation(rng, amount)
    heavy_load, ordinary = portions_of(amount, rows * top, most, lean, True), portions_of(amount, rows * top, most, lean, False)
    places = jnp.arange(amount)

    def named(tallies, rotation):
        used = int((tallies > 0).sum())
        fixed = max(1, used // 4)
        moved = fixed + (places - fixed + rotation * (used - fixed)) % max(1, amount - fixed)
        return jnp.zeros((amount,), jnp.int32).at[sequence[jnp.where(places < fixed, places, moved)]].set(jnp.asarray(tallies, jnp.int32))

    tallies = jnp.where(number % 4 == 0, named(heavy_load, number // 4), named(ordinary, number - number // 4 - 1))
    mixed = jax.random.permutation(jax.random.fold_in(own, 3), amount)
    giver, taker = mixed[0:amount // 2 * 2:2], mixed[1:amount // 2 * 2:2]
    room = jnp.minimum(tallies[giver] - 1, most - tallies[taker]) // 2
    room = jnp.where((giver == sequence[0]) | (taker == sequence[0]) | (tallies[taker] == 0), 0, jnp.maximum(room, 0))
    moved = jax.random.randint(jax.random.fold_in(own, 4), (amount // 2,), 0, 1 << 20) % (room + 1)
    tallies = tallies.at[giver].add(-moved).at[taker].add(moved)
    members = jnp.searchsorted(jnp.cumsum(tallies), jnp.arange(rows * top), side="right").astype(jnp.int32)
    grid = members.reshape(top, rows).T
    grid = grid[jax.random.permutation(jax.random.fold_in(own, 1), rows)]
    rotation = jax.random.randint(jax.random.fold_in(own, 2), (rows, 1), 0, top)
    return jnp.take_along_axis(grid, (jnp.arange(top)[None, :] + rotation) % top, axis=1)


def portions_of(amount, total, bound, slope, full):
    portions = [(1 << 20) // math.isqrt(standing ** slope) + 1 for standing in range(1, amount + 1)]
    largest = bound if full else min(bound, max(-(-total // amount), total * portions[0] // sum(portions)))
    least = 1 if total - largest >= amount - 1 else 0
    holding, surplus = [largest] + [least] * (amount - 1), total - largest - least * (amount - 1)
    while surplus > 0:
        candidates = [i for i in range(1, amount) if holding[i] < largest] or [i for i in range(1, amount) if holding[i] < bound]
        pool, remaining = sum([portions[i] for i in candidates]), surplus
        for i in candidates:
            more = min(bound - holding[i], max(1, remaining * portions[i] // pool), surplus)
            holding[i] = holding[i] + more
            surplus = surplus - more
    return np.array(holding)


def bell_draw(own_key, extent, deviation, limit, cuts=(), kind=jnp.bfloat16):
    values = jax.random.normal(own_key, extent, jnp.float32) * deviation
    if len(cuts) > 0:
        values = level_of(own_key, extent, cuts, -0.22, 0.18) * values
    return jnp.clip(values, min=-limit, max=limit).astype(kind)


def setup_inputs(seed: int = 0, part: int = 0) -> dict:
    key_of = jax.random.split(jax.random.key(seed), 13)
    own_keys = jax.random.split(jax.random.fold_in(key_of[12], part), 13)
    hidden_states = draw_hidden_states(jax.random.fold_in(jax.random.fold_in(key_of[12], part), 71), part)
    queries = draw_queries(jax.random.fold_in(jax.random.fold_in(key_of[12], part), 71), part)
    fresh_key_value = draw_fresh_key_value(jax.random.fold_in(jax.random.fold_in(key_of[12], part), 71), part)
    cache = bell_draw(own_keys[3], (REQUEST_COUNT, 2, CACHED_POSITIONS, KEY_VALUE_HEADS * HEAD_SIZE), 1.0, 8.0, ((0, 8), (3, 2)))
    cache_lengths = ragged_sizes(own_keys[4], REQUEST_COUNT, REQUEST_COUNT * CACHED_POSITIONS // 2, CACHED_POSITIONS, 1).astype(jnp.int32)
    out_weight = bell_draw(key_of[5], (QUERY_HEADS * HEAD_SIZE, D), 0.125, 1.0, ((0, 2), (1, 8)))
    router_weight = bell_draw(key_of[6], (D, EXPERTS), D ** -0.5, 0.125, ((0, 2),))
    expert_weights = bell_draw(key_of[7], (EXPERTS, 3, D, FFW), (2 * FFW) ** -0.5, 0.21875, ((0, 8), (2, 2)))
    expert_ids_keys = jax.random.split(jax.random.fold_in(own_keys[8], 1), 2 * BLOCK_TOKENS // REQUEST_TOKENS)
    expert_ids_turns = jax.random.permutation(jax.random.fold_in(own_keys[8], 3), 2 * BLOCK_TOKENS // REQUEST_TOKENS)
    expert_ids = jax.vmap(lambda own, number: deal_out(jax.random.fold_in(own_keys[8], 2), own, number, REQUEST_TOKENS, EXPERTS, TOP, CAP, 2))(expert_ids_keys, expert_ids_turns).reshape((2, BLOCK_TOKENS, TOP))
    old_slots = draw_old_slots(jax.random.fold_in(key_of[12], 71), part)
    new_slots = draw_new_slots(jax.random.fold_in(key_of[12], 71), part)
    moved_experts = draw_moved_experts(jax.random.fold_in(key_of[12], 71), part)
    return dict(hidden_states=hidden_states, queries=queries, fresh_key_value=fresh_key_value, cache=cache, cache_lengths=cache_lengths, out_weight=out_weight, router_weight=router_weight, expert_weights=expert_weights, expert_ids=expert_ids, old_slots=old_slots, new_slots=new_slots, moved_experts=moved_experts)


def lookup(entries, wanted_keys):
    return lax.optimization_barrier(jnp.sum(jnp.where(wanted_keys[..., None] == jnp.arange(entries.shape[0], dtype=jnp.int32), entries, 0), -1)).astype(jnp.int32)

def slot_source(old_slots, new_slots, moved_experts):
    slots_all = jnp.arange(EXPERTS, dtype=jnp.int32)
    new_moved = lookup(new_slots, moved_experts)
    old_moved = lookup(old_slots, moved_experts)
    matches = slots_all[:, None] == new_moved[None, :]
    return jnp.where(matches.any(1), lax.optimization_barrier(jnp.sum(jnp.where(matches, old_moved[None, :], 0), 1)), slots_all).astype(jnp.int32)

def attend_request(packed):
    query_portion, new_part, cached, length = packed
    row_total = query_portion.shape[1]
    key_matrix = jnp.concatenate([cached[0], new_part[0, :, 0], new_part[1, :, 0]], 0)
    value_matrix = jnp.concatenate([cached[1], new_part[0, :, 1], new_part[1, :, 1]], 0)
    key_total = key_matrix.shape[0]
    query_group_width = QUERY_HEADS // KEY_VALUE_HEADS
    query_matrix = query_portion.reshape(2 * row_total, KEY_VALUE_HEADS, query_group_width, HEAD_SIZE).astype(jnp.float32)
    attention_scores = jnp.einsum('meqt,wet->eqmw', query_matrix, key_matrix.reshape(key_total, KEY_VALUE_HEADS, HEAD_SIZE).astype(jnp.float32)) * HEAD_SIZE ** (-0.5)
    position = jnp.arange(key_total, dtype=jnp.int32)[None, :]
    row_index = jnp.arange(2 * row_total, dtype=jnp.int32)[:, None]
    visible = jnp.where(position < CACHED_POSITIONS, position < length, position - CACHED_POSITIONS <= row_index)
    attention_scores = jnp.where(visible, attention_scores, jnp.float32(-1e+30))
    largest = lax.optimization_barrier(jnp.max(attention_scores, -1, keepdims=True))
    weights = jnp.where(visible, jnp.exp(attention_scores - largest), jnp.float32(0.0))
    route_probability = (weights / lax.optimization_barrier(jnp.sum(weights, -1, keepdims=True))).astype(jnp.bfloat16)
    layer_result = jnp.einsum('qizo,oqx->zqix', route_probability.astype(jnp.float32), value_matrix.reshape(key_total, KEY_VALUE_HEADS, HEAD_SIZE).astype(jnp.float32))
    return layer_result.reshape(2 * row_total, QUERY_HEADS * HEAD_SIZE).astype(jnp.bfloat16)

def expert_block(token_rows, weight):
    row_total = token_rows.shape[0]
    pieces = token_rows.reshape(row_total, N_TP, QUARTER).astype(jnp.float32)
    gate_up_w = weight[:2].reshape(2, N_TP, QUARTER, FFW).astype(jnp.float32)
    partial_value = jnp.einsum('rqc,gqcf->rgqf', pieces, gate_up_w)
    rounded = lax.optimization_barrier(partial_value.astype(jnp.bfloat16)).astype(jnp.float32)
    summed = lax.optimization_barrier(jnp.sum(rounded, 2))
    hidden = (jax.nn.silu(summed[:, 0]) * summed[:, 1]).astype(jnp.bfloat16)
    return jnp.dot(hidden, weight[2].T, preferred_element_type=jnp.float32).astype(jnp.bfloat16)

def mix_block(normed_rows, resid_rows, routed, combine, slot_of_expert, expert_weights):
    expert_marks = (routed[:, :, None] == jnp.arange(EXPERTS, dtype=jnp.int32)[None, None, :]).any(1).astype(jnp.int32)
    grouped = expert_marks.reshape(REQUEST_COUNT, REQUEST_TOKENS, EXPERTS)
    before = (jnp.cumsum(grouped, 1) - grouped).reshape(BLOCK_TOKENS, EXPERTS)
    slot_rank = jnp.take_along_axis(before, routed, 1).astype(jnp.int32)
    block_of = (jnp.arange(BLOCK_TOKENS, dtype=jnp.int32) // REQUEST_TOKENS)[:, None]
    slot_width = REQUEST_COUNT * CAP
    buffer_row = ((routed * REQUEST_COUNT + block_of) * CAP + slot_rank).astype(jnp.int32)
    token_source = jnp.repeat(jnp.arange(BLOCK_TOKENS, dtype=jnp.int32), TOP)
    token_table = jnp.zeros((EXPERTS * slot_width,), jnp.int32).at[buffer_row.reshape(-1)].set(token_source)
    token_table = token_table.reshape(EXPERTS, slot_width)

    def run_expert(expert):
        token_rows = normed_rows[token_table[expert]]
        return expert_block(token_rows, expert_weights[slot_of_expert[expert]])
    outputs = lax.map(run_expert, jnp.arange(EXPERTS, dtype=jnp.int32))
    gathered = outputs.reshape(EXPERTS * slot_width, D)[buffer_row.reshape(-1)].reshape(BLOCK_TOKENS, TOP, D)
    mixed_rows = resid_rows.astype(jnp.float32) + lax.optimization_barrier(jnp.sum(combine[:, :, None] * gathered.astype(jnp.float32), 1))
    return mixed_rows.astype(jnp.bfloat16)

def reference(hidden_states, queries, fresh_key_value, cache, cache_lengths, out_weight, router_weight, expert_weights, expert_ids, old_slots, new_slots, moved_experts):
    query_parts = queries.reshape(2, REQUEST_COUNT, REQUEST_TOKENS, QUERY_HEADS * HEAD_SIZE).transpose(1, 0, 2, 3)
    fresh_pieces_list = fresh_key_value.reshape(2, REQUEST_COUNT, REQUEST_TOKENS, 2, KEY_VALUE_HEADS * HEAD_SIZE).transpose(1, 0, 2, 3, 4)
    attention = lax.map(attend_request, (query_parts, fresh_pieces_list, cache, cache_lengths))
    attention = attention.reshape(REQUEST_COUNT, 2, REQUEST_TOKENS, QUERY_HEADS * HEAD_SIZE).transpose(1, 0, 2, 3).reshape(2 * BLOCK_TOKENS, QUERY_HEADS * HEAD_SIZE)
    attn_out = jnp.dot(attention, out_weight, preferred_element_type=jnp.float32)
    residual = (hidden_states.reshape(2 * BLOCK_TOKENS, D).astype(jnp.float32) + attn_out).astype(jnp.bfloat16)
    wide = residual.astype(jnp.float32)
    squares = lax.optimization_barrier(jnp.sum(wide * wide, 1))
    normed = (wide * lax.rsqrt(squares / D + 1e-06)[:, None]).astype(jnp.bfloat16)
    logits = jnp.dot(normed, router_weight, preferred_element_type=jnp.float32)
    routed = expert_ids.reshape(2 * BLOCK_TOKENS, TOP)
    selected = jnp.take_along_axis(logits, routed, 1)
    raised = jnp.exp(selected)
    combine = raised / lax.optimization_barrier(jnp.sum(raised, 1, keepdims=True))
    first_mix = mix_block(normed[:BLOCK_TOKENS], residual[:BLOCK_TOKENS], routed[:BLOCK_TOKENS], combine[:BLOCK_TOKENS], old_slots, expert_weights)
    source = slot_source(old_slots, new_slots, moved_experts)
    second_slot = lookup(source, new_slots)
    second_mix = mix_block(normed[BLOCK_TOKENS:], residual[BLOCK_TOKENS:], routed[BLOCK_TOKENS:], combine[BLOCK_TOKENS:], second_slot, expert_weights)
    return jnp.stack([first_mix, second_mix])
```

```python
import jax
import jax.numpy as jnp
from jax import lax
from jax.sharding import PartitionSpec as P

D = 2048
HEAD_SIZE = 128


def lookup(entries, wanted_keys):
    return jnp.sum(
        jnp.where(
            wanted_keys[..., None] == jnp.arange(entries.shape[0], dtype=jnp.int32), entries, 0
        ),
        -1,
    )


def attend_local(queries, fresh_key_value, cache, cache_lengths):
    tokens_dev = queries.shape[1]
    kv_heads = fresh_key_value.shape[3] // HEAD_SIZE
    query_group_width = queries.shape[2] // HEAD_SIZE // kv_heads
    key_matrix = jnp.concatenate(
        [cache[0, 0], fresh_key_value[0, :, 0], fresh_key_value[1, :, 0]], 0
    )
    value_matrix = jnp.concatenate(
        [cache[0, 1], fresh_key_value[0, :, 1], fresh_key_value[1, :, 1]], 0
    )
    key_total = key_matrix.shape[0]
    context = cache.shape[2]
    query_matrix = queries.reshape(2 * tokens_dev, kv_heads, query_group_width, HEAD_SIZE)
    attention_scores = jnp.einsum(
        "meqt,wet->eqmw",
        query_matrix,
        key_matrix.reshape(key_total, kv_heads, HEAD_SIZE),
        preferred_element_type=jnp.float32,
    ) * HEAD_SIZE ** (-0.5)
    position = jnp.arange(key_total, dtype=jnp.int32)[None, :]
    row_index = jnp.arange(2 * tokens_dev, dtype=jnp.int32)[:, None]
    visible = jnp.where(
        position < context, position < cache_lengths[0], position - context <= row_index
    )
    attention_scores = jnp.where(visible, attention_scores, jnp.float32(-1e30))
    largest = jnp.max(attention_scores, -1, keepdims=True)
    weights = jnp.where(visible, jnp.exp(attention_scores - largest), jnp.float32(0.0))
    route_probability = (weights / jnp.sum(weights, -1, keepdims=True)).astype(jnp.bfloat16)
    layer_result = jnp.einsum(
        "qizo,oqx->zqix",
        route_probability,
        value_matrix.reshape(key_total, kv_heads, HEAD_SIZE),
        preferred_element_type=jnp.float32,
    )
    return layer_result.reshape(2 * tokens_dev, -1).astype(jnp.bfloat16)


def run_slots(weights, received):
    gate_up = jnp.einsum(
        "secq,egqf->secgf", received, weights[:, :2], preferred_element_type=jnp.float32
    )
    summed = lax.psum(gate_up.astype(jnp.bfloat16), "tp").astype(jnp.float32)
    hidden = (jax.nn.silu(summed[:, :, :, 0]) * summed[:, :, :, 1]).astype(jnp.bfloat16)
    layer_result = jnp.einsum(
        "secf,eqf->secq", hidden, weights[:, 2], preferred_element_type=jnp.float32
    ).astype(jnp.bfloat16)
    return lax.all_to_all(layer_result, "ep", split_axis=0, concat_axis=0, tiled=True)


def mix_block(normed_rows, resid_rows, routed, combine, slot_table, weights, capacity, groups):
    tokens_dev, top_count = routed.shape
    experts = slot_table.shape[0]
    local_slots = weights.shape[0]
    quarter = normed_rows.shape[1]
    slot_index = lookup(slot_table, routed)
    picked_mask = routed[:, :, None] == jnp.arange(experts, dtype=jnp.int32)[None, None, :]
    expert_marks = picked_mask.any(1).astype(jnp.bfloat16)
    earlier = (jnp.arange(tokens_dev)[:, None] > jnp.arange(tokens_dev)[None, :]).astype(
        jnp.bfloat16
    )
    before = jnp.dot(earlier, expert_marks, preferred_element_type=jnp.float32)
    slot_rank = jnp.sum(jnp.where(picked_mask, before[:, None, :], 0.0), -1).astype(jnp.int32)
    buffer_row = (slot_index * capacity + slot_rank).reshape(-1)
    buffer_rows = (
        jnp.zeros((groups * local_slots * capacity, quarter), jnp.bfloat16)
        .at[buffer_row]
        .set(jnp.repeat(normed_rows, top_count, axis=0))
    )
    outgoing = buffer_rows.reshape(groups, local_slots, capacity, quarter)
    returned = run_slots(
        weights, lax.all_to_all(outgoing, "ep", split_axis=0, concat_axis=0, tiled=True)
    )
    gathered = returned.reshape(-1, quarter)[buffer_row].reshape(tokens_dev, top_count, quarter)
    mixed_rows = resid_rows.astype(jnp.float32) + jnp.sum(
        combine[:, :, None] * gathered.astype(jnp.float32), 1
    )
    return mixed_rows.astype(jnp.bfloat16)


def gathered_experts(normed, resid, routed, combine, slot_table, weights):
    tokens_dev, quarter = normed.shape
    experts = slot_table.shape[0]
    local_slots = weights.shape[0]
    groups = lax.axis_size("ep")
    slot_index = lookup(slot_table, routed)
    slots = jnp.arange(experts, dtype=jnp.int32)
    by_slot = jnp.sum(
        jnp.where(slot_index[:, :, None] == slots, combine[:, :, None], 0.0), 1
    )
    rows = lax.all_gather(normed, "ep", axis=0, tiled=True)
    shares = lax.all_to_all(
        by_slot.reshape(tokens_dev, groups, local_slots).transpose(1, 0, 2),
        "ep",
        split_axis=0,
        concat_axis=0,
        tiled=True,
    ).reshape(groups * tokens_dev, local_slots)
    gate_up = jnp.einsum(
        "rq,egqf->regf", rows, weights[:, :2], preferred_element_type=jnp.float32
    ).astype(jnp.bfloat16)
    half = lax.psum_scatter(gate_up, "tp", scatter_dimension=0, tiled=True).astype(jnp.float32)
    hidden = (jax.nn.silu(half[:, :, 0]) * half[:, :, 1]).astype(jnp.bfloat16)
    hidden = lax.all_gather(hidden, "tp", axis=0, tiled=True)
    total = 0.0
    for slot in range(local_slots):
        out = jnp.dot(
            hidden[:, slot], weights[slot, 2].T, preferred_element_type=jnp.float32
        ).astype(jnp.bfloat16)
        total = total + shares[:, slot, None] * out.astype(jnp.float32)
    mixed = lax.psum_scatter(
        total.astype(jnp.bfloat16), "ep", scatter_dimension=0, tiled=True
    ).astype(jnp.float32)
    return (resid.astype(jnp.float32) + mixed).astype(jnp.bfloat16)


def per_device(
    hidden_states,
    queries,
    fresh_key_value,
    cache,
    cache_lengths,
    out_weight,
    router_weight,
    expert_weights,
    expert_ids,
    old_slots,
    new_slots,
    moved_experts,
):
    tokens_dev = hidden_states.shape[1]
    quarter = hidden_states.shape[2]
    experts = router_weight.shape[1]
    top_count = expert_ids.shape[2]
    groups = lax.axis_size("ep")
    local_slots = expert_weights.shape[0]
    capacity = min(tokens_dev, 3 * tokens_dev * top_count // (2 * experts))
    attention = attend_local(queries, fresh_key_value, cache, cache_lengths)
    head_terms = jnp.dot(
        attention,
        lax.all_gather(out_weight, "ep", axis=1, tiled=True),
        preferred_element_type=jnp.float32,
    )
    attn_out = lax.psum_scatter(
        head_terms.astype(jnp.bfloat16), "tp", scatter_dimension=1, tiled=True
    ).astype(jnp.float32)
    residual = (
        hidden_states.reshape(2 * tokens_dev, quarter).astype(jnp.float32) + attn_out
    ).astype(jnp.bfloat16)
    wide = residual.astype(jnp.float32)
    squares = lax.psum(jnp.sum(wide * wide, 1), "tp")
    normed = (wide * lax.rsqrt(squares / D + 1e-06)[:, None]).astype(jnp.bfloat16)
    logits = lax.psum(
        jnp.dot(normed, router_weight, preferred_element_type=jnp.float32).astype(jnp.bfloat16),
        "tp",
    ).astype(jnp.float32)
    routed = expert_ids.reshape(2 * tokens_dev, top_count)
    selected = jnp.sum(
        jnp.where(
            routed[:, :, None] == jnp.arange(experts, dtype=jnp.int32)[None, None, :],
            logits[:, None, :],
            0.0,
        ),
        -1,
    )
    raised = jnp.exp(selected)
    combine = raised / jnp.sum(raised, 1, keepdims=True)
    if groups * tokens_dev <= groups * local_slots * capacity:
        mixed = gathered_experts(normed, residual, routed, combine, old_slots, expert_weights)
        return mixed.reshape(2, tokens_dev, quarter)
    outputs = []
    for lower in (0, tokens_dev):
        upper = lower + tokens_dev
        outputs.append(
            mix_block(
                normed[lower:upper],
                residual[lower:upper],
                routed[lower:upper],
                combine[lower:upper],
                old_slots,
                expert_weights,
                capacity,
                groups,
            )
        )
    return jnp.stack(outputs)


def solution(mesh):
    return jax.shard_map(
        per_device,
        mesh=mesh,
        in_specs=(
            P(None, ("rep", "ep"), "tp"),
            P(None, ("rep", "ep"), "tp"),
            P(None, ("rep", "ep"), None, "tp"),
            P(("rep", "ep"), None, None, "tp"),
            P(("rep", "ep")),
            P("tp", "ep"),
            P("tp", None),
            P("ep", None, "tp", None),
            P(None, ("rep", "ep"), None),
            P(),
            P(),
            P(),
        ),
        out_specs=P(None, ("rep", "ep"), "tp"),
        check_vma=False,
    )
```

```python
import jax
import jax.numpy as jnp
from jax import lax
from jax.sharding import PartitionSpec as P

D = 2048
HEAD_SIZE = 128


def lookup(entries, wanted_keys):
    return jnp.sum(
        jnp.where(
            wanted_keys[..., None] == jnp.arange(entries.shape[0], dtype=jnp.int32), entries, 0
        ),
        -1,
    )


def attend_local(queries, fresh_key_value, cache, cache_lengths):
    tokens_dev = queries.shape[1]
    kv_heads = fresh_key_value.shape[3] // HEAD_SIZE
    query_group_width = queries.shape[2] // HEAD_SIZE // kv_heads
    key_matrix = jnp.concatenate(
        [cache[0, 0], fresh_key_value[0, :, 0], fresh_key_value[1, :, 0]], 0
    )
    value_matrix = jnp.concatenate(
        [cache[0, 1], fresh_key_value[0, :, 1], fresh_key_value[1, :, 1]], 0
    )
    key_total = key_matrix.shape[0]
    context = cache.shape[2]
    query_matrix = queries.reshape(2 * tokens_dev, kv_heads, query_group_width, HEAD_SIZE)
    attention_scores = jnp.einsum(
        "meqt,wet->eqmw",
        query_matrix,
        key_matrix.reshape(key_total, kv_heads, HEAD_SIZE),
        preferred_element_type=jnp.float32,
    ) * HEAD_SIZE ** (-0.5)
    position = jnp.arange(key_total, dtype=jnp.int32)[None, :]
    row_index = jnp.arange(2 * tokens_dev, dtype=jnp.int32)[:, None]
    visible = jnp.where(
        position < context, position < cache_lengths[0], position - context <= row_index
    )
    attention_scores = jnp.where(visible, attention_scores, jnp.float32(-1e30))
    largest = jnp.max(attention_scores, -1, keepdims=True)
    weights = jnp.where(visible, jnp.exp(attention_scores - largest), jnp.float32(0.0))
    route_probability = (weights / jnp.sum(weights, -1, keepdims=True)).astype(jnp.bfloat16)
    layer_result = jnp.einsum(
        "qizo,oqx->zqix",
        route_probability,
        value_matrix.reshape(key_total, kv_heads, HEAD_SIZE),
        preferred_element_type=jnp.float32,
    )
    return layer_result.reshape(2 * tokens_dev, -1).astype(jnp.bfloat16)


def run_slots(weights, received):
    gate_up = jnp.einsum(
        "secq,egqf->secgf", received, weights[:, :2], preferred_element_type=jnp.float32
    )
    summed = lax.psum(gate_up.astype(jnp.bfloat16), "tp").astype(jnp.float32)
    hidden = (jax.nn.silu(summed[:, :, :, 0]) * summed[:, :, :, 1]).astype(jnp.bfloat16)
    layer_result = jnp.einsum(
        "secf,eqf->secq", hidden, weights[:, 2], preferred_element_type=jnp.float32
    ).astype(jnp.bfloat16)
    return lax.all_to_all(layer_result, "ep", split_axis=0, concat_axis=0, tiled=True)


def mix_block(normed_rows, resid_rows, routed, combine, slot_table, weights, capacity, groups):
    tokens_dev, top_count = routed.shape
    experts = slot_table.shape[0]
    local_slots = weights.shape[0]
    quarter = normed_rows.shape[1]
    slot_index = lookup(slot_table, routed)
    picked_mask = routed[:, :, None] == jnp.arange(experts, dtype=jnp.int32)[None, None, :]
    expert_marks = picked_mask.any(1).astype(jnp.bfloat16)
    earlier = (jnp.arange(tokens_dev)[:, None] > jnp.arange(tokens_dev)[None, :]).astype(
        jnp.bfloat16
    )
    before = jnp.dot(earlier, expert_marks, preferred_element_type=jnp.float32)
    slot_rank = jnp.sum(jnp.where(picked_mask, before[:, None, :], 0.0), -1).astype(jnp.int32)
    buffer_row = (slot_index * capacity + slot_rank).reshape(-1)
    buffer_rows = (
        jnp.zeros((groups * local_slots * capacity, quarter), jnp.bfloat16)
        .at[buffer_row]
        .set(jnp.repeat(normed_rows, top_count, axis=0))
    )
    outgoing = buffer_rows.reshape(groups, local_slots, capacity, quarter)
    returned = run_slots(
        weights, lax.all_to_all(outgoing, "ep", split_axis=0, concat_axis=0, tiled=True)
    )
    gathered = returned.reshape(-1, quarter)[buffer_row].reshape(tokens_dev, top_count, quarter)
    mixed_rows = resid_rows.astype(jnp.float32) + jnp.sum(
        combine[:, :, None] * gathered.astype(jnp.float32), 1
    )
    return mixed_rows.astype(jnp.bfloat16)


def swap(value):
    return lax.ppermute(value, "tp", [(0, 1), (1, 0)])


def both_halves(value, axis):
    other = swap(value)
    first = lax.axis_index("tp") == 0
    return jnp.concatenate(
        [jnp.where(first, value, other), jnp.where(first, other, value)], axis
    )


def pick(table, index):
    return lax.dynamic_index_in_dim(table, index, 0, keepdims=False)


def gathered_layer(
    attention, hidden_states, out_weight, router_weight, weights, routed, slot_table
):
    tokens_dev, width = attention.shape[0], hidden_states.shape[1]
    experts = slot_table.shape[0]
    local_slots = weights.shape[0]
    groups = lax.axis_size("ep")
    mine = lax.axis_index("tp")
    theirs = 1 - mine
    own_gate_up = pick(weights, mine)[:2]
    sent_gate_up = swap(pick(weights, theirs)[:2])
    first = mine == 0
    gate_up_weight = jnp.concatenate(
        [
            jnp.where(first, own_gate_up, sent_gate_up),
            jnp.where(first, sent_gate_up, own_gate_up),
        ],
        1,
    )
    hidden_full = both_halves(hidden_states, 1)
    router_full = both_halves(router_weight, 0)
    head_terms = jnp.dot(
        attention,
        lax.all_gather(out_weight, "ep", axis=1, tiled=True),
        preferred_element_type=jnp.float32,
    ).astype(jnp.bfloat16)
    attn_out = head_terms.astype(jnp.float32) + swap(head_terms).astype(jnp.float32)
    residual = (hidden_full.astype(jnp.float32) + attn_out).astype(jnp.bfloat16)
    wide = residual.astype(jnp.float32)
    squares = jnp.sum(wide * wide, 1)
    normed = (wide * lax.rsqrt(squares / D + 1e-06)[:, None]).astype(jnp.bfloat16)
    rows = lax.all_gather(normed, "ep", axis=0, tiled=True)
    logits = jnp.dot(normed, router_full, preferred_element_type=jnp.float32)
    slot_of = lookup(slot_table, routed)
    marks = routed[:, :, None] == jnp.arange(experts, dtype=jnp.int32)
    raised = jnp.where(marks.any(1), jnp.exp(logits), 0.0)
    combine = raised / jnp.sum(raised, 1, keepdims=True)
    picked = jnp.sum(jnp.where(marks, combine[:, None, :], 0.0), 2)
    by_slot = jnp.sum(
        jnp.where(
            slot_of[:, :, None] == jnp.arange(experts, dtype=jnp.int32), picked[:, :, None], 0.0
        ),
        1,
    )
    shares = lax.all_gather(by_slot, "ep", axis=0, tiled=True)
    local = jnp.arange(experts, dtype=jnp.int32)[None, :] - lax.axis_index("ep") * local_slots
    own_share = jnp.sum(jnp.where(local == mine, shares, 0.0), 1, keepdims=True)
    their_share = jnp.sum(jnp.where(local == theirs, shares, 0.0), 1, keepdims=True)
    gate = jnp.dot(rows, gate_up_weight[0], preferred_element_type=jnp.float32)
    up = jnp.dot(rows, gate_up_weight[1], preferred_element_type=jnp.float32)
    hidden = (jax.nn.silu(gate) * up).astype(jnp.bfloat16)
    their_hidden = swap(hidden)

    def down(value, slot):
        return lax.dot_general(
            value, slot, (((1,), (1,)), ((), ())), preferred_element_type=jnp.float32
        )

    total = own_share * down(hidden, pick(weights, mine)[2]) + their_share * down(
        their_hidden, pick(weights, theirs)[2]
    )
    mixed = lax.psum_scatter(
        total.astype(jnp.bfloat16), "ep", scatter_dimension=0, tiled=True
    ).astype(jnp.float32)
    own_residual = jnp.where(first, residual[:, :width], residual[:, width:])
    return (own_residual.astype(jnp.float32) + mixed).astype(jnp.bfloat16)


def per_device(
    hidden_states,
    queries,
    fresh_key_value,
    cache,
    cache_lengths,
    out_weight,
    router_weight,
    expert_weights,
    expert_ids,
    old_slots,
    new_slots,
    moved_experts,
):
    tokens_dev = hidden_states.shape[1]
    quarter = hidden_states.shape[2]
    experts = router_weight.shape[1]
    top_count = expert_ids.shape[2]
    groups = lax.axis_size("ep")
    local_slots = expert_weights.shape[0]
    capacity = min(tokens_dev, 3 * tokens_dev * top_count // (2 * experts))
    attention = attend_local(queries, fresh_key_value, cache, cache_lengths)
    routed = expert_ids.reshape(2 * tokens_dev, top_count)
    if (
        tokens_dev <= local_slots * capacity
        and lax.axis_size("tp") == 2
        and local_slots == 2
    ):
        mixed = gathered_layer(
            attention,
            hidden_states.reshape(2 * tokens_dev, quarter),
            out_weight,
            router_weight,
            expert_weights,
            routed,
            old_slots,
        )
        return mixed.reshape(2, tokens_dev, quarter)
    head_terms = jnp.dot(
        attention,
        lax.all_gather(out_weight, "ep", axis=1, tiled=True),
        preferred_element_type=jnp.float32,
    )
    attn_out = lax.psum_scatter(
        head_terms.astype(jnp.bfloat16), "tp", scatter_dimension=1, tiled=True
    ).astype(jnp.float32)
    residual = (
        hidden_states.reshape(2 * tokens_dev, quarter).astype(jnp.float32) + attn_out
    ).astype(jnp.bfloat16)
    wide = residual.astype(jnp.float32)
    squares = lax.psum(jnp.sum(wide * wide, 1), "tp")
    normed = (wide * lax.rsqrt(squares / D + 1e-06)[:, None]).astype(jnp.bfloat16)
    logits = lax.psum(
        jnp.dot(normed, router_weight, preferred_element_type=jnp.float32).astype(jnp.bfloat16),
        "tp",
    ).astype(jnp.float32)
    selected = jnp.sum(
        jnp.where(
            routed[:, :, None] == jnp.arange(experts, dtype=jnp.int32)[None, None, :],
            logits[:, None, :],
            0.0,
        ),
        -1,
    )
    raised = jnp.exp(selected)
    combine = raised / jnp.sum(raised, 1, keepdims=True)
    outputs = []
    for lower in (0, tokens_dev):
        upper = lower + tokens_dev
        outputs.append(
            mix_block(
                normed[lower:upper],
                residual[lower:upper],
                routed[lower:upper],
                combine[lower:upper],
                old_slots,
                expert_weights,
                capacity,
                groups,
            )
        )
    return jnp.stack(outputs)


def solution(mesh):
    return jax.shard_map(
        per_device,
        mesh=mesh,
        in_specs=(
            P(None, ("rep", "ep"), "tp"),
            P(None, ("rep", "ep"), "tp"),
            P(None, ("rep", "ep"), None, "tp"),
            P(("rep", "ep"), None, None, "tp"),
            P(("rep", "ep")),
            P("tp", "ep"),
            P("tp", None),
            P("ep", None, "tp", None),
            P(None, ("rep", "ep"), None),
            P(),
            P(),
            P(),
        ),
        out_specs=P(None, ("rep", "ep"), "tp"),
        check_vma=False,
    )
```

```python
import jax
import jax.numpy as jnp
from jax import lax
from jax.sharding import PartitionSpec as P

D = 2048
HEAD_SIZE = 128
PIECES = 2
CHUNKS = 2


def lookup(entries, wanted_keys):
    return jnp.sum(
        jnp.where(
            wanted_keys[..., None] == jnp.arange(entries.shape[0], dtype=jnp.int32), entries, 0
        ),
        -1,
    )


def attend_local(queries, fresh_key_value, cache, cache_lengths):
    tokens_dev = queries.shape[1]
    kv_heads = fresh_key_value.shape[3] // HEAD_SIZE
    query_group_width = queries.shape[2] // HEAD_SIZE // kv_heads
    key_matrix = jnp.concatenate(
        [cache[0, 0], fresh_key_value[0, :, 0], fresh_key_value[1, :, 0]], 0
    )
    value_matrix = jnp.concatenate(
        [cache[0, 1], fresh_key_value[0, :, 1], fresh_key_value[1, :, 1]], 0
    )
    key_total = key_matrix.shape[0]
    context = cache.shape[2]
    query_matrix = queries.reshape(2 * tokens_dev, kv_heads, query_group_width, HEAD_SIZE)
    attention_scores = jnp.einsum(
        "meqt,wet->eqmw",
        query_matrix,
        key_matrix.reshape(key_total, kv_heads, HEAD_SIZE),
        preferred_element_type=jnp.float32,
    ) * HEAD_SIZE ** (-0.5)
    position = jnp.arange(key_total, dtype=jnp.int32)[None, :]
    row_index = jnp.arange(2 * tokens_dev, dtype=jnp.int32)[:, None]
    visible = jnp.where(
        position < context, position < cache_lengths[0], position - context <= row_index
    )
    attention_scores = jnp.where(visible, attention_scores, jnp.float32(-1e30))
    largest = jnp.max(attention_scores, -1, keepdims=True)
    weights = jnp.where(visible, jnp.exp(attention_scores - largest), jnp.float32(0.0))
    route_probability = (weights / jnp.sum(weights, -1, keepdims=True)).astype(jnp.bfloat16)
    layer_result = jnp.einsum(
        "qizo,oqx->zqix",
        route_probability,
        value_matrix.reshape(key_total, kv_heads, HEAD_SIZE),
        preferred_element_type=jnp.float32,
    )
    return layer_result.reshape(2 * tokens_dev, -1).astype(jnp.bfloat16)


def run_slots(weights, received):
    gate_up = jnp.einsum(
        "secq,egqf->secgf", received, weights[:, :2], preferred_element_type=jnp.float32
    )
    summed = lax.psum(gate_up.astype(jnp.bfloat16), "tp").astype(jnp.float32)
    hidden = (jax.nn.silu(summed[:, :, :, 0]) * summed[:, :, :, 1]).astype(jnp.bfloat16)
    layer_result = jnp.einsum(
        "secf,eqf->secq", hidden, weights[:, 2], preferred_element_type=jnp.float32
    ).astype(jnp.bfloat16)
    return lax.all_to_all(layer_result, "ep", split_axis=0, concat_axis=0, tiled=True)


def mix_block(normed_rows, resid_rows, routed, combine, slot_table, weights, capacity, groups):
    tokens_dev, top_count = routed.shape
    experts = slot_table.shape[0]
    local_slots = weights.shape[0]
    quarter = normed_rows.shape[1]
    slot_index = lookup(slot_table, routed)
    picked_mask = routed[:, :, None] == jnp.arange(experts, dtype=jnp.int32)[None, None, :]
    expert_marks = picked_mask.any(1).astype(jnp.bfloat16)
    earlier = (jnp.arange(tokens_dev)[:, None] > jnp.arange(tokens_dev)[None, :]).astype(
        jnp.bfloat16
    )
    before = jnp.dot(earlier, expert_marks, preferred_element_type=jnp.float32)
    slot_rank = jnp.sum(jnp.where(picked_mask, before[:, None, :], 0.0), -1).astype(jnp.int32)
    buffer_row = (slot_index * capacity + slot_rank).reshape(-1)
    buffer_rows = (
        jnp.zeros((groups * local_slots * capacity, quarter), jnp.bfloat16)
        .at[buffer_row]
        .set(jnp.repeat(normed_rows, top_count, axis=0))
    )
    outgoing = buffer_rows.reshape(groups, local_slots, capacity, quarter)
    returned = run_slots(
        weights, lax.all_to_all(outgoing, "ep", split_axis=0, concat_axis=0, tiled=True)
    )
    gathered = returned.reshape(-1, quarter)[buffer_row].reshape(tokens_dev, top_count, quarter)
    mixed_rows = resid_rows.astype(jnp.float32) + jnp.sum(
        combine[:, :, None] * gathered.astype(jnp.float32), 1
    )
    return mixed_rows.astype(jnp.bfloat16)


def swap(value):
    return lax.ppermute(value, "tp", [(0, 1), (1, 0)])


def both_halves(value, axis):
    other = swap(value)
    first = lax.axis_index("tp") == 0
    return jnp.concatenate(
        [jnp.where(first, value, other), jnp.where(first, other, value)], axis
    )


def pick(table, index):
    return lax.dynamic_index_in_dim(table, index, 0, keepdims=False)


def gathered_layer(
    attention, hidden_states, out_weight, router_weight, weights, routed, slot_table
):
    tokens_dev, width = attention.shape[0], hidden_states.shape[1]
    experts = slot_table.shape[0]
    local_slots = weights.shape[0]
    groups = lax.axis_size("ep")
    mine = lax.axis_index("tp")
    theirs = 1 - mine
    own_gate_up = pick(weights, mine)[:2]
    sent_gate_up = swap(pick(weights, theirs)[:2])
    first = mine == 0
    gate_up_weight = jnp.concatenate(
        [
            jnp.where(first, own_gate_up, sent_gate_up),
            jnp.where(first, sent_gate_up, own_gate_up),
        ],
        1,
    )
    hidden_full = both_halves(hidden_states, 1)
    router_full = both_halves(router_weight, 0)
    routed_all = lax.all_gather(routed, "ep", axis=0)
    attention, gate_up_weight, hidden_full, router_full, routed_all = lax.optimization_barrier(
        (attention, gate_up_weight, hidden_full, router_full, routed_all)
    )
    slots = jnp.arange(experts, dtype=jnp.int32)
    marks = (routed_all[:, :, :, None] == slots).any(2)
    base_slot = lax.axis_index("ep") * local_slots
    columns = out_weight.shape[1] // PIECES
    parts = []
    for piece in range(PIECES):
        block = lax.all_gather(
            out_weight[:, piece * columns : (piece + 1) * columns], "ep", axis=1, tiled=True
        )
        terms = jnp.dot(attention, block, preferred_element_type=jnp.float32).astype(jnp.bfloat16)
        summed = terms.astype(jnp.float32) + swap(terms).astype(jnp.float32)
        parts.append(summed.reshape(tokens_dev, groups, columns))
    attn_out = jnp.stack(parts, 2).reshape(tokens_dev, 2 * width)
    residual = (hidden_full.astype(jnp.float32) + attn_out).astype(jnp.bfloat16)
    wide = residual.astype(jnp.float32)
    squares = jnp.sum(wide * wide, 1)
    normed = (wide * lax.rsqrt(squares / D + 1e-06)[:, None]).astype(jnp.bfloat16)
    chunk = tokens_dev // CHUNKS
    gathered = [
        lax.all_gather(normed[lower : lower + chunk], "ep", axis=0, tiled=True)
        for lower in range(0, tokens_dev, chunk)
    ]
    def down(value, slot):
        return lax.dot_general(
            value, slot, (((1,), (1,)), ((), ())), preferred_element_type=jnp.float32
        )

    own_down = pick(weights, mine)[2]
    their_down = pick(weights, theirs)[2]
    mixed = []
    for index, rows in enumerate(gathered):
        span = slice(index * chunk, (index + 1) * chunk)
        gate = jnp.dot(rows, gate_up_weight[0], preferred_element_type=jnp.float32)
        up = jnp.dot(rows, gate_up_weight[1], preferred_element_type=jnp.float32)
        hidden = (jax.nn.silu(gate) * up).astype(jnp.bfloat16)
        their_hidden = swap(hidden)
        logits = jnp.dot(rows, router_full, preferred_element_type=jnp.float32)
        raised = jnp.where(marks[:, span].reshape(-1, experts), jnp.exp(logits), 0.0)
        combine = raised / jnp.sum(raised, 1, keepdims=True)
        own_share = jnp.sum(
            jnp.where(slot_table == base_slot + mine, combine, 0.0), 1, keepdims=True
        )
        their_share = jnp.sum(
            jnp.where(slot_table == base_slot + theirs, combine, 0.0), 1, keepdims=True
        )
        total = own_share * down(hidden, own_down) + their_share * down(their_hidden, their_down)
        total = total.astype(jnp.bfloat16)
        if index + 1 < len(gathered):
            total, gathered[index + 1] = lax.optimization_barrier((total, gathered[index + 1]))
        mixed.append(lax.psum_scatter(total, "ep", scatter_dimension=0, tiled=True))
    mixed = jnp.concatenate(mixed, 0).astype(jnp.float32)
    own_residual = jnp.where(first, residual[:, :width], residual[:, width:])
    return (own_residual.astype(jnp.float32) + mixed).astype(jnp.bfloat16)


def per_device(
    hidden_states,
    queries,
    fresh_key_value,
    cache,
    cache_lengths,
    out_weight,
    router_weight,
    expert_weights,
    expert_ids,
    old_slots,
    new_slots,
    moved_experts,
):
    tokens_dev = hidden_states.shape[1]
    quarter = hidden_states.shape[2]
    experts = router_weight.shape[1]
    top_count = expert_ids.shape[2]
    groups = lax.axis_size("ep")
    local_slots = expert_weights.shape[0]
    capacity = min(tokens_dev, 3 * tokens_dev * top_count // (2 * experts))
    attention = attend_local(queries, fresh_key_value, cache, cache_lengths)
    routed = expert_ids.reshape(2 * tokens_dev, top_count)
    if (
        tokens_dev <= local_slots * capacity
        and lax.axis_size("tp") == 2
        and local_slots == 2
    ):
        mixed = gathered_layer(
            attention,
            hidden_states.reshape(2 * tokens_dev, quarter),
            out_weight,
            router_weight,
            expert_weights,
            routed,
            old_slots,
        )
        return mixed.reshape(2, tokens_dev, quarter)
    head_terms = jnp.dot(
        attention,
        lax.all_gather(out_weight, "ep", axis=1, tiled=True),
        preferred_element_type=jnp.float32,
    )
    attn_out = lax.psum_scatter(
        head_terms.astype(jnp.bfloat16), "tp", scatter_dimension=1, tiled=True
    ).astype(jnp.float32)
    residual = (
        hidden_states.reshape(2 * tokens_dev, quarter).astype(jnp.float32) + attn_out
    ).astype(jnp.bfloat16)
    wide = residual.astype(jnp.float32)
    squares = lax.psum(jnp.sum(wide * wide, 1), "tp")
    normed = (wide * lax.rsqrt(squares / D + 1e-06)[:, None]).astype(jnp.bfloat16)
    logits = lax.psum(
        jnp.dot(normed, router_weight, preferred_element_type=jnp.float32).astype(jnp.bfloat16),
        "tp",
    ).astype(jnp.float32)
    selected = jnp.sum(
        jnp.where(
            routed[:, :, None] == jnp.arange(experts, dtype=jnp.int32)[None, None, :],
            logits[:, None, :],
            0.0,
        ),
        -1,
    )
    raised = jnp.exp(selected)
    combine = raised / jnp.sum(raised, 1, keepdims=True)
    outputs = []
    for lower in (0, tokens_dev):
        upper = lower + tokens_dev
        outputs.append(
            mix_block(
                normed[lower:upper],
                residual[lower:upper],
                routed[lower:upper],
                combine[lower:upper],
                old_slots,
                expert_weights,
                capacity,
                groups,
            )
        )
    return jnp.stack(outputs)


def solution(mesh):
    return jax.shard_map(
        per_device,
        mesh=mesh,
        in_specs=(
            P(None, ("rep", "ep"), "tp"),
            P(None, ("rep", "ep"), "tp"),
            P(None, ("rep", "ep"), None, "tp"),
            P(("rep", "ep"), None, None, "tp"),
            P(("rep", "ep")),
            P("tp", "ep"),
            P("tp", None),
            P("ep", None, "tp", None),
            P(None, ("rep", "ep"), None),
            P(),
            P(),
            P(),
        ),
        out_specs=P(None, ("rep", "ep"), "tp"),
        check_vma=False,
    )
```

```python
import jax
import jax.numpy as jnp
from jax import lax
from jax.sharding import PartitionSpec as P

D = 2048
HEAD_SIZE = 128


def lookup(entries, wanted_keys):
    return jnp.sum(
        jnp.where(
            wanted_keys[..., None] == jnp.arange(entries.shape[0], dtype=jnp.int32), entries, 0
        ),
        -1,
    )


def attend_local(queries, fresh_key_value, cache, cache_lengths):
    tokens_dev = queries.shape[1]
    kv_heads = fresh_key_value.shape[3] // HEAD_SIZE
    query_group_width = queries.shape[2] // HEAD_SIZE // kv_heads
    key_matrix = jnp.concatenate(
        [cache[0, 0], fresh_key_value[0, :, 0], fresh_key_value[1, :, 0]], 0
    )
    value_matrix = jnp.concatenate(
        [cache[0, 1], fresh_key_value[0, :, 1], fresh_key_value[1, :, 1]], 0
    )
    key_total = key_matrix.shape[0]
    context = cache.shape[2]
    query_matrix = queries.reshape(2 * tokens_dev, kv_heads, query_group_width, HEAD_SIZE)
    attention_scores = jnp.einsum(
        "meqt,wet->eqmw",
        query_matrix,
        key_matrix.reshape(key_total, kv_heads, HEAD_SIZE),
        preferred_element_type=jnp.float32,
    ) * HEAD_SIZE ** (-0.5)
    position = jnp.arange(key_total, dtype=jnp.int32)[None, :]
    row_index = jnp.arange(2 * tokens_dev, dtype=jnp.int32)[:, None]
    visible = jnp.where(
        position < context, position < cache_lengths[0], position - context <= row_index
    )
    attention_scores = jnp.where(visible, attention_scores, jnp.float32(-1e30))
    largest = jnp.max(attention_scores, -1, keepdims=True)
    weights = jnp.where(visible, jnp.exp(attention_scores - largest), jnp.float32(0.0))
    route_probability = (weights / jnp.sum(weights, -1, keepdims=True)).astype(jnp.bfloat16)
    layer_result = jnp.einsum(
        "qizo,oqx->zqix",
        route_probability,
        value_matrix.reshape(key_total, kv_heads, HEAD_SIZE),
        preferred_element_type=jnp.float32,
    )
    return layer_result.reshape(2 * tokens_dev, -1).astype(jnp.bfloat16)


def run_slots(weights, received):
    gate_up = jnp.einsum(
        "secq,egqf->secgf", received, weights[:, :2], preferred_element_type=jnp.float32
    )
    summed = lax.psum(gate_up.astype(jnp.bfloat16), "tp").astype(jnp.float32)
    hidden = (jax.nn.silu(summed[:, :, :, 0]) * summed[:, :, :, 1]).astype(jnp.bfloat16)
    layer_result = jnp.einsum(
        "secf,eqf->secq", hidden, weights[:, 2], preferred_element_type=jnp.float32
    ).astype(jnp.bfloat16)
    return lax.all_to_all(layer_result, "ep", split_axis=0, concat_axis=0, tiled=True)


def mix_block(normed_rows, resid_rows, routed, combine, slot_table, weights, capacity, groups):
    tokens_dev, top_count = routed.shape
    experts = slot_table.shape[0]
    local_slots = weights.shape[0]
    quarter = normed_rows.shape[1]
    slot_index = lookup(slot_table, routed)
    picked_mask = routed[:, :, None] == jnp.arange(experts, dtype=jnp.int32)[None, None, :]
    expert_marks = picked_mask.any(1).astype(jnp.bfloat16)
    earlier = (jnp.arange(tokens_dev)[:, None] > jnp.arange(tokens_dev)[None, :]).astype(
        jnp.bfloat16
    )
    before = jnp.dot(earlier, expert_marks, preferred_element_type=jnp.float32)
    slot_rank = jnp.sum(jnp.where(picked_mask, before[:, None, :], 0.0), -1).astype(jnp.int32)
    buffer_row = (slot_index * capacity + slot_rank).reshape(-1)
    buffer_rows = (
        jnp.zeros((groups * local_slots * capacity, quarter), jnp.bfloat16)
        .at[buffer_row]
        .set(jnp.repeat(normed_rows, top_count, axis=0))
    )
    outgoing = buffer_rows.reshape(groups, local_slots, capacity, quarter)
    returned = run_slots(
        weights, lax.all_to_all(outgoing, "ep", split_axis=0, concat_axis=0, tiled=True)
    )
    gathered = returned.reshape(-1, quarter)[buffer_row].reshape(tokens_dev, top_count, quarter)
    mixed_rows = resid_rows.astype(jnp.float32) + jnp.sum(
        combine[:, :, None] * gathered.astype(jnp.float32), 1
    )
    return mixed_rows.astype(jnp.bfloat16)


def swap(value):
    return lax.ppermute(value, "tp", [(0, 1), (1, 0)])


def both_halves(value, axis):
    other = swap(value)
    first = lax.axis_index("tp") == 0
    return jnp.concatenate(
        [jnp.where(first, value, other), jnp.where(first, other, value)], axis
    )


def pick(table, index):
    return lax.dynamic_index_in_dim(table, index, 0, keepdims=False)


def gathered_layer(
    attention, hidden_states, out_weight, router_weight, weights, routed, slot_table
):
    tokens_dev, width = attention.shape[0], hidden_states.shape[1]
    experts = slot_table.shape[0]
    local_slots = weights.shape[0]
    mine = lax.axis_index("tp")
    theirs = 1 - mine
    projection = lax.all_gather(out_weight, "ep", axis=1, tiled=True)
    own_gate_up = pick(weights, mine)[:2]
    sent_gate_up = swap(pick(weights, theirs)[:2])
    first = mine == 0
    gate_up_weight = jnp.concatenate(
        [
            jnp.where(first, own_gate_up, sent_gate_up),
            jnp.where(first, sent_gate_up, own_gate_up),
        ],
        1,
    )
    hidden_full = both_halves(hidden_states, 1)
    router_full = both_halves(router_weight, 0)
    routed_all = lax.all_gather(routed, "ep", axis=0, tiled=True)
    attention, gate_up_weight, hidden_full, router_full, routed_all = lax.optimization_barrier(
        (attention, gate_up_weight, hidden_full, router_full, routed_all)
    )
    slots = jnp.arange(experts, dtype=jnp.int32)
    marks = (routed_all[:, :, None] == slots).any(1)
    base_slot = lax.axis_index("ep") * local_slots
    head_terms = jnp.dot(
        attention, projection, preferred_element_type=jnp.float32
    ).astype(jnp.bfloat16)
    attn_out = head_terms.astype(jnp.float32) + swap(head_terms).astype(jnp.float32)
    residual = (hidden_full.astype(jnp.float32) + attn_out).astype(jnp.bfloat16)
    wide = residual.astype(jnp.float32)
    squares = jnp.sum(wide * wide, 1)
    normed = (wide * lax.rsqrt(squares / D + 1e-06)[:, None]).astype(jnp.bfloat16)
    rows = lax.all_gather(normed, "ep", axis=0, tiled=True)

    def down(value, slot):
        return lax.dot_general(
            value, slot, (((1,), (1,)), ((), ())), preferred_element_type=jnp.float32
        )

    own_down = pick(weights, mine)[2]
    their_down = pick(weights, theirs)[2]
    gate = jnp.dot(rows, gate_up_weight[0], preferred_element_type=jnp.float32)
    up = jnp.dot(rows, gate_up_weight[1], preferred_element_type=jnp.float32)
    hidden = (jax.nn.silu(gate) * up).astype(jnp.bfloat16)
    their_hidden = swap(hidden)
    logits = jnp.dot(rows, router_full, preferred_element_type=jnp.float32)
    raised = jnp.where(marks, jnp.exp(logits), 0.0)
    combine = raised / jnp.sum(raised, 1, keepdims=True)
    own_share = jnp.sum(jnp.where(slot_table == base_slot + mine, combine, 0.0), 1, keepdims=True)
    their_share = jnp.sum(
        jnp.where(slot_table == base_slot + theirs, combine, 0.0), 1, keepdims=True
    )
    total = own_share * down(hidden, own_down) + their_share * down(their_hidden, their_down)
    mixed = lax.psum_scatter(
        total.astype(jnp.bfloat16), "ep", scatter_dimension=0, tiled=True
    ).astype(jnp.float32)
    own_residual = jnp.where(first, residual[:, :width], residual[:, width:])
    return (own_residual.astype(jnp.float32) + mixed).astype(jnp.bfloat16)


def per_device(
    hidden_states,
    queries,
    fresh_key_value,
    cache,
    cache_lengths,
    out_weight,
    router_weight,
    expert_weights,
    expert_ids,
    old_slots,
    new_slots,
    moved_experts,
):
    tokens_dev = hidden_states.shape[1]
    quarter = hidden_states.shape[2]
    experts = router_weight.shape[1]
    top_count = expert_ids.shape[2]
    groups = lax.axis_size("ep")
    local_slots = expert_weights.shape[0]
    capacity = min(tokens_dev, 3 * tokens_dev * top_count // (2 * experts))
    attention = attend_local(queries, fresh_key_value, cache, cache_lengths)
    routed = expert_ids.reshape(2 * tokens_dev, top_count)
    if (
        tokens_dev <= local_slots * capacity
        and lax.axis_size("tp") == 2
        and local_slots == 2
    ):
        mixed = gathered_layer(
            attention,
            hidden_states.reshape(2 * tokens_dev, quarter),
            out_weight,
            router_weight,
            expert_weights,
            routed,
            old_slots,
        )
        return mixed.reshape(2, tokens_dev, quarter)
    head_terms = jnp.dot(
        attention,
        lax.all_gather(out_weight, "ep", axis=1, tiled=True),
        preferred_element_type=jnp.float32,
    )
    attn_out = lax.psum_scatter(
        head_terms.astype(jnp.bfloat16), "tp", scatter_dimension=1, tiled=True
    ).astype(jnp.float32)
    residual = (
        hidden_states.reshape(2 * tokens_dev, quarter).astype(jnp.float32) + attn_out
    ).astype(jnp.bfloat16)
    wide = residual.astype(jnp.float32)
    squares = lax.psum(jnp.sum(wide * wide, 1), "tp")
    normed = (wide * lax.rsqrt(squares / D + 1e-06)[:, None]).astype(jnp.bfloat16)
    logits = lax.psum(
        jnp.dot(normed, router_weight, preferred_element_type=jnp.float32).astype(jnp.bfloat16),
        "tp",
    ).astype(jnp.float32)
    selected = jnp.sum(
        jnp.where(
            routed[:, :, None] == jnp.arange(experts, dtype=jnp.int32)[None, None, :],
            logits[:, None, :],
            0.0,
        ),
        -1,
    )
    raised = jnp.exp(selected)
    combine = raised / jnp.sum(raised, 1, keepdims=True)
    outputs = []
    for lower in (0, tokens_dev):
        upper = lower + tokens_dev
        outputs.append(
            mix_block(
                normed[lower:upper],
                residual[lower:upper],
                routed[lower:upper],
                combine[lower:upper],
                old_slots,
                expert_weights,
                capacity,
                groups,
            )
        )
    return jnp.stack(outputs)


def solution(mesh):
    return jax.shard_map(
        per_device,
        mesh=mesh,
        in_specs=(
            P(None, ("rep", "ep"), "tp"),
            P(None, ("rep", "ep"), "tp"),
            P(None, ("rep", "ep"), None, "tp"),
            P(("rep", "ep"), None, None, "tp"),
            P(("rep", "ep")),
            P("tp", "ep"),
            P("tp", None),
            P("ep", None, "tp", None),
            P(None, ("rep", "ep"), None),
            P(),
            P(),
            P(),
        ),
        out_specs=P(None, ("rep", "ep"), "tp"),
        check_vma=False,
    )
```

```python
import jax
import jax.numpy as jnp
from jax import lax
from jax.sharding import PartitionSpec as P

D = 2048
HEAD_SIZE = 128


def lookup(entries, wanted_keys):
    return jnp.sum(
        jnp.where(
            wanted_keys[..., None] == jnp.arange(entries.shape[0], dtype=jnp.int32), entries, 0
        ),
        -1,
    )


def attend_local(queries, fresh_key_value, cache, cache_lengths):
    tokens_dev = queries.shape[1]
    kv_heads = fresh_key_value.shape[3] // HEAD_SIZE
    query_group_width = queries.shape[2] // HEAD_SIZE // kv_heads
    key_matrix = jnp.concatenate(
        [cache[0, 0], fresh_key_value[0, :, 0], fresh_key_value[1, :, 0]], 0
    )
    value_matrix = jnp.concatenate(
        [cache[0, 1], fresh_key_value[0, :, 1], fresh_key_value[1, :, 1]], 0
    )
    key_total = key_matrix.shape[0]
    context = cache.shape[2]
    query_matrix = queries.reshape(2 * tokens_dev, kv_heads, query_group_width, HEAD_SIZE)
    attention_scores = jnp.einsum(
        "meqt,wet->eqmw",
        query_matrix,
        key_matrix.reshape(key_total, kv_heads, HEAD_SIZE),
        preferred_element_type=jnp.float32,
    ) * HEAD_SIZE ** (-0.5)
    position = jnp.arange(key_total, dtype=jnp.int32)[None, :]
    row_index = jnp.arange(2 * tokens_dev, dtype=jnp.int32)[:, None]
    visible = jnp.where(
        position < context, position < cache_lengths[0], position - context <= row_index
    )
    attention_scores = jnp.where(visible, attention_scores, jnp.float32(-1e30))
    largest = jnp.max(attention_scores, -1, keepdims=True)
    weights = jnp.where(visible, jnp.exp(attention_scores - largest), jnp.float32(0.0))
    route_probability = (weights / jnp.sum(weights, -1, keepdims=True)).astype(jnp.bfloat16)
    layer_result = jnp.einsum(
        "qizo,oqx->zqix",
        route_probability,
        value_matrix.reshape(key_total, kv_heads, HEAD_SIZE),
        preferred_element_type=jnp.float32,
    )
    return layer_result.reshape(2 * tokens_dev, -1).astype(jnp.bfloat16)


def run_slots(weights, received):
    gate_up = jnp.einsum(
        "secq,egqf->secgf", received, weights[:, :2], preferred_element_type=jnp.float32
    )
    summed = lax.psum(gate_up.astype(jnp.bfloat16), "tp").astype(jnp.float32)
    hidden = (jax.nn.silu(summed[:, :, :, 0]) * summed[:, :, :, 1]).astype(jnp.bfloat16)
    layer_result = jnp.einsum(
        "secf,eqf->secq", hidden, weights[:, 2], preferred_element_type=jnp.float32
    ).astype(jnp.bfloat16)
    return lax.all_to_all(layer_result, "ep", split_axis=0, concat_axis=0, tiled=True)


def mix_block(normed_rows, resid_rows, routed, combine, slot_table, weights, capacity, groups):
    tokens_dev, top_count = routed.shape
    experts = slot_table.shape[0]
    local_slots = weights.shape[0]
    quarter = normed_rows.shape[1]
    slot_index = lookup(slot_table, routed)
    picked_mask = routed[:, :, None] == jnp.arange(experts, dtype=jnp.int32)[None, None, :]
    expert_marks = picked_mask.any(1).astype(jnp.bfloat16)
    earlier = (jnp.arange(tokens_dev)[:, None] > jnp.arange(tokens_dev)[None, :]).astype(
        jnp.bfloat16
    )
    before = jnp.dot(earlier, expert_marks, preferred_element_type=jnp.float32)
    slot_rank = jnp.sum(jnp.where(picked_mask, before[:, None, :], 0.0), -1).astype(jnp.int32)
    buffer_row = (slot_index * capacity + slot_rank).reshape(-1)
    buffer_rows = (
        jnp.zeros((groups * local_slots * capacity, quarter), jnp.bfloat16)
        .at[buffer_row]
        .set(jnp.repeat(normed_rows, top_count, axis=0))
    )
    outgoing = buffer_rows.reshape(groups, local_slots, capacity, quarter)
    returned = run_slots(
        weights, lax.all_to_all(outgoing, "ep", split_axis=0, concat_axis=0, tiled=True)
    )
    gathered = returned.reshape(-1, quarter)[buffer_row].reshape(tokens_dev, top_count, quarter)
    mixed_rows = resid_rows.astype(jnp.float32) + jnp.sum(
        combine[:, :, None] * gathered.astype(jnp.float32), 1
    )
    return mixed_rows.astype(jnp.bfloat16)


def swap(value):
    return lax.ppermute(value, "tp", [(0, 1), (1, 0)])


def both_halves(value, axis):
    other = swap(value)
    first = lax.axis_index("tp") == 0
    return jnp.concatenate(
        [jnp.where(first, value, other), jnp.where(first, other, value)], axis
    )


def pick(table, index):
    return lax.dynamic_index_in_dim(table, index, 0, keepdims=False)


def gathered_layer(
    attention, hidden_states, out_weight, router_weight, weights, routed, slot_table
):
    tokens_dev, width = attention.shape[0], hidden_states.shape[1]
    experts = slot_table.shape[0]
    local_slots = weights.shape[0]
    mine = lax.axis_index("tp")
    theirs = 1 - mine
    groups = lax.axis_size("ep")
    attention_all = lax.all_gather(attention, "ep", axis=0, tiled=True)
    own_gate_up = pick(weights, mine)[:2]
    sent_gate_up = swap(pick(weights, theirs)[:2])
    first = mine == 0
    gate_up_weight = jnp.concatenate(
        [
            jnp.where(first, own_gate_up, sent_gate_up),
            jnp.where(first, sent_gate_up, own_gate_up),
        ],
        1,
    )
    hidden_full = both_halves(hidden_states, 1)
    router_full = both_halves(router_weight, 0)
    routed_all = lax.all_gather(routed, "ep", axis=0, tiled=True)
    out_weight, gate_up_weight, hidden_full, router_full, routed_all = lax.optimization_barrier(
        (out_weight, gate_up_weight, hidden_full, router_full, routed_all)
    )
    slots = jnp.arange(experts, dtype=jnp.int32)
    marks = (routed_all[:, :, None] == slots).any(1)
    base_slot = lax.axis_index("ep") * local_slots
    column_terms = jnp.dot(
        attention_all, out_weight, preferred_element_type=jnp.float32
    ).astype(jnp.bfloat16)
    head_terms = lax.all_to_all(
        column_terms.reshape(groups, tokens_dev, -1), "ep", split_axis=0, concat_axis=0, tiled=True
    )
    head_terms = head_terms.transpose(1, 0, 2).reshape(tokens_dev, 2 * width)
    attn_out = head_terms.astype(jnp.float32) + swap(head_terms).astype(jnp.float32)
    residual = (hidden_full.astype(jnp.float32) + attn_out).astype(jnp.bfloat16)
    wide = residual.astype(jnp.float32)
    squares = jnp.sum(wide * wide, 1)
    normed = (wide * lax.rsqrt(squares / D + 1e-06)[:, None]).astype(jnp.bfloat16)
    rows = lax.all_gather(normed, "ep", axis=0, tiled=True)

    def down(value, slot):
        return lax.dot_general(
            value, slot, (((1,), (1,)), ((), ())), preferred_element_type=jnp.float32
        )

    own_down = pick(weights, mine)[2]
    their_down = pick(weights, theirs)[2]
    gate = jnp.dot(rows, gate_up_weight[0], preferred_element_type=jnp.float32)
    up = jnp.dot(rows, gate_up_weight[1], preferred_element_type=jnp.float32)
    hidden = (jax.nn.silu(gate) * up).astype(jnp.bfloat16)
    their_hidden = swap(hidden)
    logits = jnp.dot(rows, router_full, preferred_element_type=jnp.float32)
    raised = jnp.where(marks, jnp.exp(logits), 0.0)
    combine = raised / jnp.sum(raised, 1, keepdims=True)
    own_share = jnp.sum(jnp.where(slot_table == base_slot + mine, combine, 0.0), 1, keepdims=True)
    their_share = jnp.sum(
        jnp.where(slot_table == base_slot + theirs, combine, 0.0), 1, keepdims=True
    )
    total = own_share * down(hidden, own_down) + their_share * down(their_hidden, their_down)
    mixed = lax.psum_scatter(
        total.astype(jnp.bfloat16), "ep", scatter_dimension=0, tiled=True
    ).astype(jnp.float32)
    own_residual = jnp.where(first, residual[:, :width], residual[:, width:])
    return (own_residual.astype(jnp.float32) + mixed).astype(jnp.bfloat16)


def per_device(
    hidden_states,
    queries,
    fresh_key_value,
    cache,
    cache_lengths,
    out_weight,
    router_weight,
    expert_weights,
    expert_ids,
    old_slots,
    new_slots,
    moved_experts,
):
    tokens_dev = hidden_states.shape[1]
    quarter = hidden_states.shape[2]
    experts = router_weight.shape[1]
    top_count = expert_ids.shape[2]
    groups = lax.axis_size("ep")
    local_slots = expert_weights.shape[0]
    capacity = min(tokens_dev, 3 * tokens_dev * top_count // (2 * experts))
    attention = attend_local(queries, fresh_key_value, cache, cache_lengths)
    routed = expert_ids.reshape(2 * tokens_dev, top_count)
    if (
        tokens_dev <= local_slots * capacity
        and lax.axis_size("tp") == 2
        and local_slots == 2
    ):
        mixed = gathered_layer(
            attention,
            hidden_states.reshape(2 * tokens_dev, quarter),
            out_weight,
            router_weight,
            expert_weights,
            routed,
            old_slots,
        )
        return mixed.reshape(2, tokens_dev, quarter)
    head_terms = jnp.dot(
        attention,
        lax.all_gather(out_weight, "ep", axis=1, tiled=True),
        preferred_element_type=jnp.float32,
    )
    attn_out = lax.psum_scatter(
        head_terms.astype(jnp.bfloat16), "tp", scatter_dimension=1, tiled=True
    ).astype(jnp.float32)
    residual = (
        hidden_states.reshape(2 * tokens_dev, quarter).astype(jnp.float32) + attn_out
    ).astype(jnp.bfloat16)
    wide = residual.astype(jnp.float32)
    squares = lax.psum(jnp.sum(wide * wide, 1), "tp")
    normed = (wide * lax.rsqrt(squares / D + 1e-06)[:, None]).astype(jnp.bfloat16)
    logits = lax.psum(
        jnp.dot(normed, router_weight, preferred_element_type=jnp.float32).astype(jnp.bfloat16),
        "tp",
    ).astype(jnp.float32)
    selected = jnp.sum(
        jnp.where(
            routed[:, :, None] == jnp.arange(experts, dtype=jnp.int32)[None, None, :],
            logits[:, None, :],
            0.0,
        ),
        -1,
    )
    raised = jnp.exp(selected)
    combine = raised / jnp.sum(raised, 1, keepdims=True)
    outputs = []
    for lower in (0, tokens_dev):
        upper = lower + tokens_dev
        outputs.append(
            mix_block(
                normed[lower:upper],
                residual[lower:upper],
                routed[lower:upper],
                combine[lower:upper],
                old_slots,
                expert_weights,
                capacity,
                groups,
            )
        )
    return jnp.stack(outputs)


def solution(mesh):
    return jax.shard_map(
        per_device,
        mesh=mesh,
        in_specs=(
            P(None, ("rep", "ep"), "tp"),
            P(None, ("rep", "ep"), "tp"),
            P(None, ("rep", "ep"), None, "tp"),
            P(("rep", "ep"), None, None, "tp"),
            P(("rep", "ep")),
            P("tp", "ep"),
            P("tp", None),
            P("ep", None, "tp", None),
            P(None, ("rep", "ep"), None),
            P(),
            P(),
            P(),
        ),
        out_specs=P(None, ("rep", "ep"), "tp"),
        check_vma=False,
    )
```
